512 devices in a mesh: sky: 16 (over z), tile: 32 (over y, x, core).
Axes of the slice: x: 4, y: 4, z: 16, core: 2. Of those that a mesh axis runs over, the one named last changes fastest.
Arguments:
- science: float32 [16, 32, 2, 128, 512], P('sky', 'tile'), may hold values from -6 to 6
- inverse_variance: bfloat16 [16, 32, 2, 128, 512], P('sky', 'tile'), may hold values from 0.25 to 4
- template: bfloat16 [16, 32, 128, 512], P('sky', 'tile'), may hold values from -6 to 6
- filters: bfloat16 [8, 21], replicated, may hold values from -1.25 to 1.25
- kernel_index: int32 [20, 2], replicated, may hold values from 0 to 7
- spatial_coeff: float32 [16, 32, 2, 3, 20], P('sky', 'tile'), may hold values from -1.5 to 1.5
- visit_offset: int32 [16, 2], P('sky'), may hold values from 0 to 31
- block_count: int32 [16, 32, 2], P('sky', 'tile'), may hold values from 12 to 16, as said below
- block_owner: int32 [16, 32, 32], P('sky', 'tile'), may hold values from 0 to 31, as said below
- block_slot: int32 [16, 32, 32], P('sky', 'tile'), may hold values from 0 to 2
- coadd_sum: float32 [16, 32, 3, 4096], P('sky', 'tile'), may hold values from -18 to 18
- coadd_weight: float32 [16, 32, 3, 4096], P('sky', 'tile'), may hold values from 2 to 8
Outputs:
- difference: float32 [16, 32, 2, 128, 512], P('sky', 'tile')
- coadd: float32 [16, 32, 3, 4096], P('sky', 'tile')
The draws below stay inside these ranges and needn't reach their ends.
Inputs may be any that keep to these rules, and one draw needn't show every extreme that they name: `visit_offset`: exposure tile i of a group lies in visit v on template tile (i + offset) mod 32. `block_count`: blocks 0 to count - 1 of a tile and visit enter the coadd. `block_owner`: among the 32 blocks of one device no owner appears more than 2 times; in each sky group one owner receives exactly 2 blocks from every device of the group, their first 2 blocks.
All inputs are finite; a program needn't handle non-finite values.
Results may differ from the reference program's by a relative error of at most 0.0026.
Values may be sent and summed in bfloat16 or wider, within the bound.
No kernel may reach another device: no remote copies, remote signals or barrier semaphores. Data moves between devices by JAX's collectives and lax.ppermute only.
A program may use at most 64 MiB of HBM per device.

```python
import math
import jax
import jax.numpy as jnp
from jax import lax

H = 128
W = 512
VISITS = 2
NBASIS = 8
KERNELS = 20
TAPS = 21
HALF = 10
BS = 64
PATCH_DEV = 3
GROUPS = 16
TILES = 32
BPV = 16
NBLK = 32
CAP = 2


def draw_block_count(key, part):
    entry_total = GROUPS * TILES * VISITS
    lowered = jax.random.randint(jax.random.fold_in(key, 11), (entry_total,), 0, BPV // 4 + 1)
    counts = BPV - lowered
    chosen_spot = jax.random.randint(jax.random.fold_in(key, 12), (), 0, entry_total)
    position = jnp.arange(entry_total, dtype=jnp.int32)
    counts = jnp.where(position == chosen_spot, BPV, counts)
    counts = jnp.where(position == (chosen_spot + 1) % entry_total, BPV - BPV // 4, counts)
    return counts.reshape(GROUPS, TILES, VISITS).astype(jnp.int32)


def draw_block_owner(key, part):
    hot_owner = jax.random.randint(jax.random.fold_in(key, 21), (GROUPS, 1, 1), 0, TILES)
    pool_size = TILES * CAP
    base_owner = jnp.arange(pool_size, dtype=jnp.int32) % TILES
    device_keys = jax.random.split(jax.random.fold_in(key, 22), GROUPS * TILES)
    shuffled = jax.vmap(lambda k: jax.random.permutation(k, pool_size))(device_keys)
    owners = base_owner[shuffled].reshape(GROUPS, TILES, pool_size)
    position = jnp.arange(pool_size, dtype=jnp.int32)[None, None, :]
    score = jnp.where(owners == hot_owner, position - pool_size, position)
    ordering = jnp.argsort(score, axis=-1, stable=True)
    ordered = jnp.take_along_axis(owners, ordering, axis=-1)
    return ordered[..., :NBLK].astype(jnp.int32)


def plant(drawn, rng, smallest, largest):
    extent = drawn.shape
    place = [jax.random.randint(jax.random.fold_in(rng, axis), (), 0, extent[axis]) for axis in range(len(extent))]
    drawn = drawn.at[tuple(place)].set(smallest)
    longest = extent.index(max(extent))
    place[longest] = (place[longest] + 1) % extent[longest]
    return drawn.at[tuple(place)].set(largest)


def block_levels(stream_key, shape, shards, smallest, high):
    def one(dim, parts):
        draws = jax.random.uniform(jax.random.fold_in(jax.random.fold_in(stream_key, 6), dim), (parts,), jnp.float32, smallest / len(shards), high / len(shards))
        return jnp.repeat(jnp.exp(draws), shape[dim] // parts).reshape((-1,) + (1,) * (len(shape) - dim - 1))

    level = one(*shards[0])
    for cut in shards[1:]:
        level = level * one(*cut)
    return level


def scatter_about(stream_key, dims, spread, bound, cuts=(), kind=jnp.bfloat16):
    array = spread * jax.random.normal(stream_key, dims, jnp.float32)
    if cuts:
        array = array * block_levels(stream_key, dims, cuts, -0.22, 0.18)
    return jnp.clip(array, -bound, bound).astype(kind)


def setup_inputs(seed: int = 0) -> dict:
    key_of = jax.random.split(jax.random.key(seed), 13)
    return {
        "science": scatter_about(key_of[0], (GROUPS, TILES, VISITS, H, W), 1.0, 6.0, ((0, 16), (1, 32)), jnp.float32),
        "inverse_variance": jnp.clip(jnp.exp(math.log(4.0) - 2.7725887 * jax.random.uniform(key_of[1], (GROUPS, TILES, VISITS, H, W), jnp.float32) ** block_levels(key_of[1], (GROUPS, TILES, VISITS, H, W), ((0, 16), (1, 32)), -0.2, 0.2)), 0.25, 4.0).astype(jnp.bfloat16),
        "template": scatter_about(key_of[2], (GROUPS, TILES, H, W), 1.0, 6.0, ((0, 16), (1, 32))),
        "filters": scatter_about(key_of[3], (NBASIS, TAPS), TAPS ** -0.5, 1.25),
        "kernel_index": plant(jax.random.randint(key_of[4], (KERNELS, 2), 0, NBASIS), jax.random.fold_in(key_of[4], 1), 0, NBASIS - 1).astype(jnp.int32),
        "spatial_coeff": scatter_about(key_of[5], (GROUPS, TILES, VISITS, 3, KERNELS), 0.25, 1.5, ((0, 16), (1, 32)), jnp.float32),
        "visit_offset": plant(jax.random.randint(key_of[6], (GROUPS, VISITS), 0, TILES), jax.random.fold_in(key_of[6], 1), 0, TILES - 1).astype(jnp.int32),
        "block_count": draw_block_count(jax.random.fold_in(key_of[12], 71), 0),
        "block_owner": draw_block_owner(jax.random.fold_in(key_of[12], 71), 0),
        "block_slot": plant(jax.random.randint(key_of[9], (GROUPS, TILES, NBLK), 0, PATCH_DEV), jax.random.fold_in(key_of[9], 1), 0, PATCH_DEV - 1).astype(jnp.int32),
        "coadd_sum": scatter_about(key_of[10], (GROUPS, TILES, PATCH_DEV, BS * BS), 3.0, 18.0, ((0, 16), (1, 32)), jnp.float32),
        "coadd_weight": jnp.clip(jnp.exp(math.log(8.0) - 1.3862944 * jax.random.uniform(key_of[11], (GROUPS, TILES, PATCH_DEV, BS * BS), jnp.float32) ** block_levels(key_of[11], (GROUPS, TILES, PATCH_DEV, BS * BS), ((0, 16), (1, 32)), -0.2, 0.2)), 2.0, 8.0),
    }


def block_rows(image):
    leading = image.shape[:-3]
    lead_count = len(leading)
    pieces = image.reshape(leading + (VISITS, H // BS, BS, W // BS, BS))
    axis_order = tuple(range(lead_count)) + (lead_count, lead_count + 1, lead_count + 3, lead_count + 2, lead_count + 4)
    return jnp.transpose(pieces, axis_order).reshape(leading + (NBLK, BS * BS))


def group_update(inputs, filter_taps, kernel_index):
    science, inverse_variance, template, spatial_coeff, visit_offset, block_count, block_owner, block_slot = inputs
    tile_ids = (jnp.arange(TILES, dtype=jnp.int32)[None, :] + visit_offset[:, None]) % TILES
    aligned = jnp.transpose(template[tile_ids], (1, 0, 2, 3))
    padded = jnp.pad(aligned, ((0, 0), (0, 0), (0, 0), (HALF, HALF)))

    def row_filter(row_taps):
        running = jnp.zeros(aligned.shape, jnp.float32)
        for q in range(TAPS):
            running = running + row_taps[q] * padded[..., q:q + W].astype(jnp.float32)
        return running.astype(jnp.bfloat16)

    filtered = lax.map(row_filter, filter_taps)
    across = (2.0 * jnp.arange(W, dtype=jnp.float32) + 1.0 - W) / W
    downward = (2.0 * jnp.arange(H, dtype=jnp.float32) + 1.0 - H) / H

    def add_kernel(matched, kernel_item):
        index_pair, kernel_coeff = kernel_item
        source = filtered[index_pair[0]]
        column_taps = filter_taps[index_pair[1]]
        shifted = jnp.pad(source, ((0, 0), (0, 0), (HALF, HALF), (0, 0)))
        convolved = jnp.zeros(source.shape, jnp.float32)
        for p in range(TAPS):
            convolved = convolved + column_taps[p] * shifted[:, :, p:p + H, :].astype(jnp.float32)
        weight_map = kernel_coeff[..., 0, None, None] + kernel_coeff[..., 1, None, None] * across + kernel_coeff[..., 2, None, None] * downward[:, None]
        return matched + weight_map * convolved, None

    matched, unused = lax.scan(add_kernel, jnp.zeros(aligned.shape, jnp.float32), (kernel_index, jnp.moveaxis(spatial_coeff, -1, 0)))
    difference = science - matched
    inverse = inverse_variance.astype(jnp.float32)
    weighted = block_rows(inverse * difference)
    weight_rows = block_rows(inverse)
    row_index = jnp.arange(NBLK, dtype=jnp.int32)
    is_valid = (row_index % BPV)[None, :] < jnp.repeat(block_count, BPV, axis=1)
    row_mask = is_valid.astype(jnp.float32)[..., None]
    destination = (block_owner * PATCH_DEV + block_slot).reshape(-1)
    sums = jax.ops.segment_sum((weighted * row_mask).reshape(-1, BS * BS), destination, num_segments=TILES * PATCH_DEV)
    weights = jax.ops.segment_sum((weight_rows * row_mask).reshape(-1, BS * BS), destination, num_segments=TILES * PATCH_DEV)
    return difference, sums.reshape(TILES, PATCH_DEV, BS * BS), weights.reshape(TILES, PATCH_DEV, BS * BS)


def share_edges(totals):
    lower = jnp.concatenate([jnp.zeros_like(totals[:1, :, -1]), totals[:-1, :, -1]], axis=0)
    upper = jnp.concatenate([totals[1:, :, 0], jnp.zeros_like(totals[:1, :, 0])], axis=0)
    return totals.at[:, :, 0].add(lower).at[:, :, -1].add(upper)


def reference(science, inverse_variance, template, filters, kernel_index, spatial_coeff, visit_offset, block_count, block_owner, block_slot, coadd_sum, coadd_weight):
    filter_taps = filters.astype(jnp.float32)

    def one_group(inputs):
        return group_update(inputs, filter_taps, kernel_index)

    difference, sums, weights = lax.map(one_group, (science, inverse_variance, template, spatial_coeff, visit_offset, block_count, block_owner, block_slot))
    merged_sums = share_edges(sums)
    merged_weights = share_edges(weights)
    coadd = (coadd_sum + merged_sums) / (coadd_weight + merged_weights)
    return difference, coadd
```

```python
import jax
import jax.numpy as jnp
from jax import lax
from jax.experimental import pallas as pl
from jax.experimental.pallas import tpu as pltpu
from jax.sharding import PartitionSpec as P

TILES = 32
VISITS = 2
H = 128
W = 512
BS = 64
NB = 8
TAPS = 21
HALF = 10
LANE = 128
CB = W // LANE
NBLK = 32
PATCHES = 3
f32 = jnp.float32
bf16 = jnp.bfloat16
VMEM = pl.BlockSpec(memory_space=pltpu.VMEM)
SMEM = pl.BlockSpec(memory_space=pltpu.SMEM)


def call(kernel, outs, in_specs, cost, scratch=()):
    return pl.pallas_call(
        kernel,
        out_shape=outs,
        in_specs=in_specs,
        out_specs=jax.tree.map(lambda _: VMEM, outs),
        scratch_shapes=list(scratch),
        compiler_params=pltpu.CompilerParams(vmem_limit_bytes=48 * 2**20),
        cost_estimate=pl.CostEstimate(flops=cost[0], bytes_accessed=cost[1], transcendentals=0),
    )


def toeplitz(row, width):
    return pltpu.roll(jnp.broadcast_to(row, (LANE, width)), 0, 1, stride=1, stride_axis=0)


def prep_kernel(taps_ref, eff_ref, band_ref, hi_ref, lo_ref):
    for j in range(NB):
        band_ref[pl.ds(j * LANE, LANE), :] = toeplitz(taps_ref[j : j + 1, :], 2 * LANE).astype(bf16)
    row = lax.broadcasted_iota(jnp.int32, (H, H), 0)
    col = lax.broadcasted_iota(jnp.int32, (H, H), 1)
    inside = jnp.abs(row - col) <= HALF
    down = (2.0 * row.astype(f32) + 1.0 - H) / H
    for v in range(VISITS):
        for r in range(NB):
            base = v * 3 * NB + r
            parts = [toeplitz(eff_ref[base + t * NB : base + t * NB + 1, :], H) for t in range(3)]
            for m, value in enumerate((parts[0] + down * parts[2], parts[1])):
                value = jnp.where(inside, value, 0.0)
                high = value.astype(bf16)
                where = (v, pl.ds(m * H, H), pl.ds(r * H, H))
                hi_ref[where] = high
                lo_ref[where] = (value - high.astype(f32)).astype(bf16)


def roll_kernel(offset_ref, held_ref, out_ref):
    for v in range(VISITS):
        offset = offset_ref[0, v]
        for i in range(TILES):
            out_ref[i, pl.ds(v * 16, 16), :] = held_ref[(offset + i) & (TILES - 1)]


def main_kernel(
    place_ref, slot_ref, arrived_ref, band_ref, hi_ref, lo_ref, science_ref, inverse_ref,
    difference_ref, payload_ref, filtered_ref,
):
    payload_ref[...] = jnp.zeros_like(payload_ref)
    lane = lax.broadcasted_iota(jnp.int32, (H, LANE), 1)
    across = (2.0 * lax.broadcasted_iota(jnp.int32, (H, W), 1).astype(f32) + 1.0 - W) / W
    left = lax.broadcasted_iota(jnp.int32, (BS, LANE), 1) < BS
    left16 = lax.broadcasted_iota(jnp.int32, (16, LANE), 1) < BS
    zero = jnp.zeros((H, LANE), bf16)
    for v in range(VISITS):
        tiles = [
            jnp.concatenate(
                [arrived_ref[rb * CB + b, pl.ds(v * 16, 16), :] for rb in range(H // 16)], axis=0
            )
            for b in range(CB)
        ]
        for b in range(CB):
            after = tiles[b + 1] if b + 1 < CB else zero
            before = tiles[b - 1] if b > 0 else zero
            window = jnp.concatenate([tiles[b], jnp.where(lane < BS, after, before)], axis=1)
            rows = lax.dot_general(
                window, band_ref[...], (((1,), (1,)), ((), ())), preferred_element_type=f32
            ).astype(bf16)
            for j in range(NB):
                filtered_ref[pl.ds(j * H, H), pl.ds(b * LANE, LANE)] = rows[:, j * LANE : (j + 1) * LANE]
        filtered = filtered_ref[...]
        both = jnp.dot(hi_ref[v], filtered, preferred_element_type=f32) + jnp.dot(
            lo_ref[v], filtered, preferred_element_type=f32
        )
        difference = science_ref[v] - (both[:H] + across * both[H:])
        difference_ref[v] = difference
        inverse = inverse_ref[v].astype(f32)
        weighted = inverse * difference
        for by in range(H // BS):
            for pair in range(CB):
                cut = (slice(by * BS, (by + 1) * BS), slice(pair * LANE, (pair + 1) * LANE))
                straight, swapped = [], []
                for x in (weighted[cut], inverse[cut]):
                    straight.append(x.astype(bf16))
                    swapped.append(pltpu.roll(x, BS, 1).astype(bf16))
                straight = jnp.concatenate(straight, axis=0)
                swapped = jnp.concatenate(swapped, axis=0)
                for parity in range(2):
                    r = v * 16 + by * 8 + pair * 2 + parity
                    place = place_ref[r]
                    slot = slot_ref[r].astype(f32)

                    def put(half, data, place=place, slot=slot):
                        owner = place >> 1
                        keep = left if half == 0 else jnp.logical_not(left)
                        keep2 = jnp.concatenate([keep, keep], axis=0)
                        payload_ref[owner, pl.ds(0, 2 * BS), :] = jnp.where(
                            keep2, data, payload_ref[owner, pl.ds(0, 2 * BS), :]
                        )
                        keep16 = left16 if half == 0 else jnp.logical_not(left16)
                        payload_ref[owner, pl.ds(2 * BS, 16), :] = jnp.where(
                            keep16, jnp.full((16, LANE), slot).astype(bf16), payload_ref[owner, pl.ds(2 * BS, 16), :]
                        )

                    for half in range(2):
                        @pl.when(jnp.logical_and(place >= 0, (place & 1) == half))
                        def _(half=half):
                            put(half, straight if half == parity else swapped)


def sum_kernel(arrived_ref, total_ref):
    left = lax.broadcasted_iota(jnp.int32, (BS, LANE), 1) < BS
    sums = []
    for part in range(2):
        def body(j, acc):
            head = arrived_ref[j, pl.ds(2 * BS, 16), :].astype(f32)[:1]
            value = arrived_ref[j, pl.ds(part * BS, BS), :].astype(f32)
            return tuple(
                acc[s] + jnp.where(jnp.broadcast_to(head == s, (BS, LANE)), value, 0.0) for s in range(PATCHES)
            )
        acc = lax.fori_loop(0, TILES, body, tuple(jnp.zeros((BS, LANE), f32) for _ in range(PATCHES)), unroll=4)
        sums.append([a + pltpu.roll(a, BS, 1) for a in acc])
    for s in range(PATCHES):
        total_ref[s] = jnp.where(left, sums[0][s], sums[1][s])


def final_kernel(total_ref, low_ref, high_ref, sum_ref, weight_ref, out_ref, merged_ref):
    left = lax.broadcasted_iota(jnp.int32, (BS // 2, LANE), 1) < BS
    for s in range(PATCHES):
        merged = total_ref[s]
        if s == 0:
            merged = merged + low_ref[...]
        if s == PATCHES - 1:
            merged = merged + high_ref[...]
        merged_ref[...] = merged
        even = merged_ref[pl.ds(0, BS // 2, stride=2), :]
        odd = merged_ref[pl.ds(1, BS // 2, stride=2), :]
        value = jnp.where(left, even, pltpu.roll(odd, BS, 1))
        weight = jnp.where(left, pltpu.roll(even, BS, 1), odd)
        result = (sum_ref[s] + value) / (weight_ref[s] + weight)
        for i in range(BS // 2):
            out_ref[s : s + 1, pl.ds(i * LANE, LANE)] = result[i : i + 1, :]


def all_to_all(x):
    return lax.all_to_all(x, "tile", split_axis=0, concat_axis=0, tiled=True)


def shards(
    science,
    inverse_variance,
    template,
    filters,
    kernel_index,
    spatial_coeff,
    visit_offset,
    block_count,
    block_owner,
    block_slot,
    coadd_sum,
    coadd_weight,
):
    sds = jax.ShapeDtypeStruct
    strips = template[0, 0].reshape(H // 16, 16, CB, LANE).transpose(0, 2, 1, 3).reshape(TILES, 16, LANE)
    held = all_to_all(strips)

    taps = filters.astype(f32)
    ids = jnp.arange(NB, dtype=jnp.int32)
    row_pick = (kernel_index[:, 0, None] == ids[None, :]).astype(f32)
    column_pick = (kernel_index[:, 1, None] == ids[None, :]).astype(f32)
    column_taps = jnp.sum(column_pick[:, :, None] * taps[None], axis=1)
    coeffs = spatial_coeff[0, 0].reshape(VISITS * 3, -1)
    effective = jnp.sum(
        (coeffs[:, None, :] * row_pick.T[None])[..., None] * column_taps[None, None], axis=2
    ).reshape(VISITS * 3 * NB, TAPS)

    def centred(rows, width):
        gap = jnp.zeros((rows.shape[0], width - TAPS), f32)
        return jnp.concatenate([rows[:, HALF:], gap, rows[:, :HALF]], axis=1)

    band, hi, lo = call(
        prep_kernel,
        (
            sds((NB * LANE, 2 * LANE), bf16),
            sds((VISITS, 2 * H, NB * H), bf16),
            sds((VISITS, 2 * H, NB * H), bf16),
        ),
        [VMEM, VMEM],
        (10_000_000, 3_000_000),
    )(centred(taps, 2 * LANE), centred(effective, H))

    owners = block_owner[0, 0]
    row = jnp.arange(NBLK, dtype=jnp.int32)
    earlier = (owners[:, None] == owners[None, :]) & (row[None, :] < row[:, None])
    repeat = jnp.sum(earlier.astype(jnp.int32), axis=1)
    counted = row % (NBLK // VISITS) < jnp.repeat(block_count[0, 0], NBLK // VISITS)
    place = jnp.where(counted, 2 * owners + repeat, -1)

    outgoing = call(
        roll_kernel, sds((TILES, VISITS * 16, LANE), bf16), [SMEM, VMEM], (0, 400_000)
    )(visit_offset, held)
    arrived = all_to_all(outgoing)

    difference, payload = call(
        main_kernel,
        (sds((VISITS, H, W), f32), sds((TILES, 2 * BS + 16, LANE), bf16)),
        [SMEM, SMEM] + [VMEM] * 6,
        (2_000_000_000, 6_000_000),
        [pltpu.VMEM((NB * H, W), bf16)],
    )(place, block_slot[0, 0], arrived, band, hi, lo, science[0, 0], inverse_variance[0, 0])

    total = call(
        sum_kernel, sds((PATCHES, BS, LANE), f32), [VMEM], (10_000_000, 1_300_000)
    )(all_to_all(payload))

    count = lax.axis_size("sky")
    low = lax.ppermute(total[PATCHES - 1], "sky", [(i, i + 1) for i in range(count - 1)])
    high = lax.ppermute(total[0], "sky", [(i + 1, i) for i in range(count - 1)])
    result = call(
        final_kernel,
        sds((PATCHES, BS * BS), f32),
        [VMEM] * 5,
        (100_000, 300_000),
        [pltpu.VMEM((BS, LANE), f32)],
    )(
        total,
        low,
        high,
        coadd_sum[0, 0].reshape(PATCHES, BS // 2, LANE),
        coadd_weight[0, 0].reshape(PATCHES, BS // 2, LANE),
    )
    return (difference[None, None], result[None, None])


def solution(mesh):
    return jax.shard_map(
        shards,
        mesh=mesh,
        in_specs=(
            P("sky", "tile", None, None, None),
            P("sky", "tile", None, None, None),
            P("sky", "tile", None, None),
            P(),
            P(),
            P("sky", "tile", None, None, None),
            P("sky", None),
            P("sky", "tile", None),
            P("sky", "tile", None),
            P("sky", "tile", None),
            P("sky", "tile", None, None),
            P("sky", "tile", None, None),
        ),
        out_specs=(P("sky", "tile", None, None, None), P("sky", "tile", None, None)),
        check_vma=False,
    )
```

```python
import jax
import jax.numpy as jnp
from jax import lax
from jax.experimental.layout import Layout, with_layout_constraint
from jax.experimental import pallas as pl
from jax.experimental.pallas import tpu as pltpu
from jax.sharding import PartitionSpec as P

TILES = 32
VISITS = 2
H = 128
W = 512
BS = 64
NB = 8
TAPS = 21
HALF = 10
LANE = 128
CB = W // LANE
NBLK = 32
BPV = NBLK // VISITS
KERNELS = 20
PATCHES = 3
f32 = jnp.float32
bf16 = jnp.bfloat16
VMEM = pl.BlockSpec(memory_space=pltpu.VMEM)
SMEM = pl.BlockSpec(memory_space=pltpu.SMEM)


def call(kernel, outs, in_specs, cost, scratch=(), out_specs=None):
    return pl.pallas_call(
        kernel,
        out_shape=outs,
        in_specs=in_specs,
        out_specs=out_specs or jax.tree.map(lambda _: VMEM, outs),
        scratch_shapes=list(scratch),
        compiler_params=pltpu.CompilerParams(vmem_limit_bytes=24 * 2**20),
        cost_estimate=pl.CostEstimate(flops=cost[0], bytes_accessed=cost[1], transcendentals=0),
    )


def toeplitz(row, width):
    return pltpu.roll(jnp.broadcast_to(row, (LANE, width)), 0, 1, stride=1, stride_axis=0)


def prep_kernel(
    index_ref, owner_ref, slot_ref, count_ref, filters_ref, coeff_ref,
    band_ref, both_ref, from_ref, slots_ref, seen_ref, taps_ref, weight_ref, eff_ref,
):
    for p in range(2 * TILES):
        from_ref[p] = NBLK
        slots_ref[p] = 0
    for o in range(TILES):
        seen_ref[o] = 0
    for r in range(NBLK):
        owner = owner_ref[r]
        repeat = seen_ref[owner]
        seen_ref[owner] = repeat + 1
        place = 2 * owner + repeat
        counted = r % BPV < count_ref[r // BPV]
        from_ref[place] = jnp.where(counted, r, NBLK)
        slots_ref[place] = slot_ref[r]

    taps_ref[...] = jnp.zeros_like(taps_ref)
    taps_ref[:, pl.ds(0, TAPS)] = filters_ref[...].astype(f32)
    taps_ref[...] = pltpu.roll(taps_ref[...], 2 * LANE - HALF, 1)
    weight_ref[...] = jnp.zeros_like(weight_ref)
    for v in range(VISITS):
        weight_ref[pl.ds(3 * v, 3), pl.ds(0, KERNELS)] = coeff_ref[v]
    eff_ref[...] = jnp.zeros_like(eff_ref)
    for k in range(KERNELS):
        r, c = index_ref[0, k], index_ref[1, k]
        taps = jnp.broadcast_to(taps_ref[pl.ds(c, 1), :], (8, 2 * LANE))
        weight = jnp.broadcast_to(weight_ref[:, k : k + 1], (8, 2 * LANE))
        eff_ref[r] = eff_ref[r] + weight * taps

    for j in range(NB):
        band_ref[pl.ds(j * LANE, LANE), :] = toeplitz(taps_ref[j : j + 1, :], 2 * LANE).astype(bf16)
    row = lax.broadcasted_iota(jnp.int32, (H, H), 0)
    col = lax.broadcasted_iota(jnp.int32, (H, H), 1)
    inside = jnp.abs(row - col) <= HALF
    down = (2.0 * row.astype(f32) + 1.0 - H) / H
    for v in range(VISITS):
        for r in range(NB):
            rows = eff_ref[r]
            rows = rows[:, :LANE] + rows[:, LANE:]
            parts = [toeplitz(rows[3 * v + t : 3 * v + t + 1], H) for t in range(3)]
            for m, value in enumerate((parts[0] + down * parts[2], parts[1])):
                value = jnp.where(inside, value, 0.0)
                high = value.astype(bf16)
                both_ref[v, pl.ds(m * H, H), pl.ds(r * H, H)] = high
                both_ref[v, pl.ds((2 + m) * H, H), pl.ds(r * H, H)] = (value - high.astype(f32)).astype(bf16)


def roll_kernel(offset_ref, held_ref, out_ref):
    for v in range(VISITS):
        offset = offset_ref[0, v]
        for i in range(TILES):
            out_ref[i, pl.ds(v * 16, 16), :] = held_ref[(offset + i) & (TILES - 1)]


def spread(plane, blocks_ref, v):
    left = lax.broadcasted_iota(jnp.int32, (BS, LANE), 1) < BS
    for by in range(H // BS):
        for pair in range(CB):
            here = plane[by * BS : (by + 1) * BS, pair * LANE : (pair + 1) * LANE]
            there = pltpu.roll(here, BS, 1)
            r = v * BPV + by * (W // BS) + pair * 2
            blocks_ref[r] = jnp.where(left, here, there).astype(bf16)
            blocks_ref[r + 1] = jnp.where(left, there, here).astype(bf16)


def pack(from_ref, blocks_ref, payload_ref, top):
    left = lax.broadcasted_iota(jnp.int32, (BS, LANE), 1) < BS
    for o in range(TILES):
        payload_ref[o, pl.ds(top, BS), :] = jnp.where(
            left, blocks_ref[from_ref[2 * o]], blocks_ref[from_ref[2 * o + 1]]
        )


def main_kernel(
    from_ref, slots_ref, arrived_ref, band_ref, both_ref, science_ref, inverse_ref,
    difference_ref, payload_ref, window_ref, filtered_ref, blocks_ref, weights_ref,
):
    lane = lax.broadcasted_iota(jnp.int32, (H, LANE), 1)
    across = (2.0 * lax.broadcasted_iota(jnp.int32, (H, W), 1).astype(f32) + 1.0 - W) / W
    zero = jnp.zeros((H, LANE), bf16)
    blocks_ref[NBLK] = jnp.zeros((BS, LANE), bf16)
    weights_ref[NBLK] = jnp.zeros((BS, LANE), bf16)
    for v in range(VISITS):
        tiles = [
            jnp.concatenate(
                [arrived_ref[2 * rt + b // 2, pl.ds(v * 16 + b % 2 * 8, 8), :] for rt in range(H // 8)], axis=0
            )
            for b in range(CB)
        ]
        for b in range(CB):
            after = tiles[b + 1] if b + 1 < CB else zero
            before = tiles[b - 1] if b > 0 else zero
            rows = pl.ds((v * CB + b) * H, H)
            window_ref[rows, pl.ds(0, LANE)] = tiles[b]
            window_ref[rows, pl.ds(LANE, LANE)] = jnp.where(lane < BS, after, before)
    for jj in range(NB // 2):
        rows = lax.dot_general(
            window_ref[...],
            band_ref[pl.ds(jj * 2 * LANE, 2 * LANE), :],
            (((1,), (1,)), ((), ())),
            preferred_element_type=f32,
        ).astype(bf16)
        for v in range(VISITS):
            for b in range(CB):
                for j in range(2):
                    top = (v * CB + b) * H
                    filtered_ref[v, pl.ds((2 * jj + j) * H, H), pl.ds(b * LANE, LANE)] = rows[
                        top : top + H, j * LANE : (j + 1) * LANE
                    ]
    for v in range(VISITS):
        both = jnp.dot(both_ref[v], filtered_ref[v], preferred_element_type=f32)
        both = both[: 2 * H] + both[2 * H :]
        difference = science_ref[v] - (both[:H] + across * both[H:])
        difference_ref[v] = difference
        inverse = inverse_ref[v].astype(f32)
        spread(inverse, weights_ref, v)
        spread(inverse * difference, blocks_ref, v)
    pack(from_ref, blocks_ref, payload_ref, 0)
    pack(from_ref, weights_ref, payload_ref, BS)
    left = lax.broadcasted_iota(jnp.int32, (8, LANE), 1) < BS
    for o in range(TILES):
        slots = [jnp.full((8, LANE), slots_ref[2 * o + k], jnp.int32) for k in range(2)]
        payload_ref[o, pl.ds(2 * BS, 8), :] = jnp.where(left, slots[0], slots[1]).astype(f32).astype(bf16)


def sum_kernel(arrived_ref, total_ref):
    left = lax.broadcasted_iota(jnp.int32, (BS, LANE), 1) < BS
    sums = []
    for part in range(2):
        def body(j, acc):
            head = arrived_ref[j, pl.ds(2 * BS, 8), :].astype(f32)[:1]
            value = arrived_ref[j, pl.ds(part * BS, BS), :].astype(f32)
            return tuple(
                acc[s] + jnp.where(jnp.broadcast_to(head == s, (BS, LANE)), value, 0.0) for s in range(PATCHES)
            )

        acc = lax.fori_loop(0, TILES, body, tuple(jnp.zeros((BS, LANE), f32) for _ in range(PATCHES)), unroll=4)
        sums.append([a + pltpu.roll(a, BS, 1) for a in acc])
    for s in range(PATCHES):
        total_ref[s] = jnp.where(left, sums[0][s], sums[1][s])


def final_kernel(total_ref, low_ref, high_ref, sum_ref, weight_ref, out_ref, merged_ref):
    left = lax.broadcasted_iota(jnp.int32, (BS // 2, LANE), 1) < BS
    for s in range(PATCHES):
        merged = total_ref[s]
        if s == 0:
            merged = merged + low_ref[...]
        if s == PATCHES - 1:
            merged = merged + high_ref[...]
        merged_ref[...] = merged
        even = merged_ref[pl.ds(0, BS // 2, stride=2), :]
        odd = merged_ref[pl.ds(1, BS // 2, stride=2), :]
        value = jnp.where(left, even, pltpu.roll(odd, BS, 1))
        weight = jnp.where(left, pltpu.roll(even, BS, 1), odd)
        out_ref[s] = (sum_ref[s] + value) / (weight_ref[s] + weight)


def all_to_all(x):
    return lax.all_to_all(x, "tile", split_axis=0, concat_axis=0, tiled=True)


def shards(
    science,
    inverse_variance,
    template,
    filters,
    kernel_index,
    spatial_coeff,
    visit_offset,
    block_count,
    block_owner,
    block_slot,
    coadd_sum,
    coadd_weight,
):
    sds = jax.ShapeDtypeStruct
    tiles = template[0, 0].reshape(H // 8, 8, CB, LANE)
    tiles = with_layout_constraint(tiles, Layout(major_to_minor=(0, 2, 1, 3)))
    held = all_to_all(tiles.transpose(0, 2, 1, 3).reshape(TILES, 16, LANE))
    outgoing = call(
        roll_kernel, sds((TILES, VISITS * 16, LANE), bf16), [SMEM, VMEM], (0, 400_000)
    )(visit_offset, held)

    outgoing, index = lax.optimization_barrier((outgoing, kernel_index.T))
    band, both, origin, slots = call(
        prep_kernel,
        (
            sds((NB * LANE, 2 * LANE), bf16),
            sds((VISITS, 4 * H, NB * H), bf16),
            sds((2 * TILES,), jnp.int32),
            sds((2 * TILES,), jnp.int32),
        ),
        [SMEM, SMEM, SMEM, SMEM, VMEM, VMEM],
        (10_000_000, 3_000_000),
        [
            pltpu.SMEM((TILES,), jnp.int32),
            pltpu.VMEM((NB, 2 * LANE), f32),
            pltpu.VMEM((8, LANE), f32),
            pltpu.VMEM((NB, 8, 2 * LANE), f32),
        ],
        (VMEM, VMEM, SMEM, SMEM),
    )(index, block_owner[0, 0], block_slot[0, 0], block_count[0, 0], filters, spatial_coeff[0, 0])
    arrived = all_to_all(outgoing)

    blocks = pltpu.VMEM((NBLK + 1, BS, LANE), bf16)
    difference, payload = call(
        main_kernel,
        (sds((VISITS, H, W), f32), sds((TILES, 2 * BS + 8, LANE), bf16)),
        [SMEM, SMEM] + [VMEM] * 5,
        (2_000_000_000, 6_000_000),
        [
            pltpu.VMEM((VISITS * CB * H, 2 * LANE), bf16),
            pltpu.VMEM((VISITS, NB * H, W), bf16),
            blocks,
            blocks,
        ],
    )(origin, slots, arrived, band, both, science[0, 0], inverse_variance[0, 0])

    total = call(
        sum_kernel, sds((PATCHES, BS, LANE), f32), [VMEM], (5_000_000, 1_300_000)
    )(all_to_all(payload))

    count = lax.axis_size("sky")
    low = lax.ppermute(total[PATCHES - 1], "sky", [(i, i + 1) for i in range(count - 1)])
    high = lax.ppermute(total[0], "sky", [(i + 1, i) for i in range(count - 1)])
    result = call(
        final_kernel,
        sds((PATCHES, BS // 2, LANE), f32),
        [VMEM] * 5,
        (100_000, 300_000),
        [pltpu.VMEM((BS, LANE), f32)],
    )(
        total,
        low,
        high,
        coadd_sum[0, 0].reshape(PATCHES, BS // 2, LANE),
        coadd_weight[0, 0].reshape(PATCHES, BS // 2, LANE),
    )
    return (difference[None, None], result.reshape(1, 1, PATCHES, BS * BS))


def solution(mesh):
    return jax.shard_map(
        shards,
        mesh=mesh,
        in_specs=(
            P("sky", "tile", None, None, None),
            P("sky", "tile", None, None, None),
            P("sky", "tile", None, None),
            P(),
            P(),
            P("sky", "tile", None, None, None),
            P("sky", None),
            P("sky", "tile", None),
            P("sky", "tile", None),
            P("sky", "tile", None),
            P("sky", "tile", None, None),
            P("sky", "tile", None, None),
        ),
        out_specs=(P("sky", "tile", None, None, None), P("sky", "tile", None, None)),
        check_vma=False,
    )
```

```python
import jax
import jax.numpy as jnp
from jax import lax
from jax.experimental.layout import Layout, with_layout_constraint
from jax.experimental import pallas as pl
from jax.experimental.pallas import tpu as pltpu
from jax.sharding import PartitionSpec as P

TILES = 32
VISITS = 2
H = 128
W = 512
BS = 64
NB = 8
TAPS = 21
HALF = 10
LANE = 128
CB = W // LANE
NBLK = 32
BPV = NBLK // VISITS
KERNELS = 20
PATCHES = 3
f32 = jnp.float32
bf16 = jnp.bfloat16
VMEM = pl.BlockSpec(memory_space=pltpu.VMEM)
ANY = pl.BlockSpec(memory_space=pl.ANY)
SMEM = pl.BlockSpec(memory_space=pltpu.SMEM)


def call(kernel, outs, in_specs, cost, scratch=(), out_specs=None):
    return pl.pallas_call(
        kernel,
        out_shape=outs,
        in_specs=in_specs,
        out_specs=out_specs or jax.tree.map(lambda _: VMEM, outs),
        scratch_shapes=list(scratch),
        compiler_params=pltpu.CompilerParams(vmem_limit_bytes=24 * 2**20),
        cost_estimate=pl.CostEstimate(flops=cost[0], bytes_accessed=cost[1], transcendentals=0),
    )


def toeplitz(row, width):
    return pltpu.roll(jnp.broadcast_to(row, (LANE, width)), 0, 1, stride=1, stride_axis=0)


def effective_taps(index_ref, filters_ref, coeff_ref, taps_ref, weight_ref):
    taps_ref[...] = jnp.zeros_like(taps_ref)
    taps_ref[pl.ds(0, NB), pl.ds(0, TAPS)] = filters_ref[...].astype(f32)
    taps_ref[pl.ds(0, NB), :] = pltpu.roll(taps_ref[pl.ds(0, NB), :], 2 * LANE - HALF, 1)
    weight_ref[...] = jnp.zeros_like(weight_ref)
    for v in range(VISITS):
        weight_ref[pl.ds(3 * v, 3), pl.ds(0, KERNELS)] = coeff_ref[:, v, :]
    weight_ref[pl.ds(8, 2), pl.ds(0, KERNELS)] = index_ref[...].astype(f32)
    weight = weight_ref[pl.ds(0, 8), :]
    rows = jnp.broadcast_to(weight_ref[8:9, :], (8, LANE))
    columns = jnp.broadcast_to(weight_ref[9:10, :], (LANE, LANE))
    picked = jnp.concatenate([jnp.where(rows == r, weight, 0.0) for r in range(NB)], axis=0)
    one = (lax.broadcasted_iota(jnp.int32, (LANE, LANE), 0).astype(f32) == columns).astype(f32)
    by_column = lax.dot_general(
        picked, one, (((1,), (1,)), ((), ())), precision=lax.Precision.HIGHEST, preferred_element_type=f32
    )
    taps = taps_ref[:, pl.ds(0, LANE)] + taps_ref[:, pl.ds(LANE, LANE)]
    return jnp.dot(by_column, taps, precision=lax.Precision.HIGHEST, preferred_element_type=f32)


def column_bands(eff_ref, both_ref):
    row = lax.broadcasted_iota(jnp.int32, (H, H), 0)
    inside = jnp.abs(row - lax.broadcasted_iota(jnp.int32, (H, H), 1)) <= HALF
    down = (2.0 * row.astype(f32) + 1.0 - H) / H

    def body(n, carry):
        v, r = n // NB, n % NB
        cols = pl.ds(pl.multiple_of(r * H, H), H)
        wide = [jnp.broadcast_to(eff_ref[pl.ds(8 * r + 3 * v + t, 1), :], (H, H)) for t in range(3)]
        for m, value in enumerate((wide[0] + down * wide[2], wide[1])):
            value = jnp.where(inside, pltpu.roll(value, 0, 1, stride=1, stride_axis=0), 0.0)
            high = value.astype(bf16)
            both_ref[v, pl.ds(m * H, H), cols] = high
            both_ref[v, pl.ds((2 + m) * H, H), cols] = (value - high.astype(f32)).astype(bf16)
        return carry

    lax.fori_loop(0, VISITS * NB, body, 0)


def pack_weights(from_ref, slots_ref, inverse_ref, payload_ref, blocks_ref):
    left = lax.broadcasted_iota(jnp.int32, (BS, LANE), 1) < BS
    blocks_ref[NBLK] = jnp.zeros((BS, LANE), bf16)

    def spread_pair(n, carry):
        v, by, pair = n // 8, n // CB % 2, n % CB
        here = inverse_ref[
            v, pl.ds(pl.multiple_of(by * BS, BS), BS), pl.ds(pl.multiple_of(pair * LANE, LANE), LANE)
        ].astype(f32)
        there = pltpu.roll(here, BS, 1)
        blocks_ref[2 * n] = jnp.where(left, here, there).astype(bf16)
        blocks_ref[2 * n + 1] = jnp.where(left, there, here).astype(bf16)
        return carry

    lax.fori_loop(0, NBLK // 2, spread_pair, 0)

    def place(o, carry):
        payload_ref[o, pl.ds(0, BS), :] = jnp.where(
            left, blocks_ref[from_ref[2 * o]], blocks_ref[from_ref[2 * o + 1]]
        )
        slots = [jnp.full((8, LANE), slots_ref[2 * o + k], jnp.int32) for k in range(2)]
        payload_ref[o, pl.ds(BS, 8), :] = jnp.where(left[:8], slots[0], slots[1]).astype(f32).astype(bf16)
        return carry

    lax.fori_loop(0, TILES, place, 0, unroll=2)


def prep_kernel(
    owner_ref, slot_ref, count_ref, index_ref, filters_ref, coeff_ref,
    band_ref, eff_ref, from_ref, slots_ref, seen_ref, taps_ref, weight_ref,
):
    def clear(o, carry):
        from_ref[2 * o] = NBLK
        from_ref[2 * o + 1] = NBLK
        slots_ref[2 * o] = 0
        slots_ref[2 * o + 1] = 0
        seen_ref[o] = 0
        return carry

    lax.fori_loop(0, TILES, clear, 0, unroll=4)
    eff_ref[...] = effective_taps(index_ref, filters_ref, coeff_ref, taps_ref, weight_ref)
    for v in range(VISITS):
        count = count_ref[v]

        def put(i, carry, v=v, count=count):
            r = v * BPV + i
            owner = owner_ref[r]
            repeat = seen_ref[owner]
            seen_ref[owner] = repeat + 1
            place = 2 * owner + repeat
            from_ref[place] = jnp.where(i < count, r, NBLK)
            slots_ref[place] = slot_ref[r]
            return carry

        lax.fori_loop(0, BPV, put, 0, unroll=2)

    def band(j, carry):
        rows = pl.ds(pl.multiple_of(j * LANE, LANE), LANE)
        band_ref[rows, :] = toeplitz(taps_ref[pl.ds(j, 1), :], 2 * LANE).astype(bf16)
        return carry

    lax.fori_loop(0, NB, band, 0, unroll=2)


def second_prep_kernel(from_ref, slots_ref, eff_ref, inverse_ref, both_ref, payload_ref, blocks_ref):
    column_bands(eff_ref, both_ref)
    pack_weights(from_ref, slots_ref, inverse_ref, payload_ref, blocks_ref)


def spread(plane, blocks_ref, v):
    left = lax.broadcasted_iota(jnp.int32, (BS, LANE), 1) < BS
    for by in range(H // BS):
        for pair in range(CB):
            here = plane[by * BS : (by + 1) * BS, pair * LANE : (pair + 1) * LANE]
            there = pltpu.roll(here, BS, 1)
            r = v * BPV + by * (W // BS) + pair * 2
            blocks_ref[r] = jnp.where(left, here, there).astype(bf16)
            blocks_ref[r + 1] = jnp.where(left, there, here).astype(bf16)


def main_kernel(
    from_ref, tile0_ref, tile1_ref, band_ref, both_ref, weights_hbm, science_hbm, inverse_hbm,
    difference_hbm, payload_hbm, window_ref, filtered_ref, blocks_ref,
    science_ref, inverse_ref, difference_ref, payload_ref, sems,
):
    def load(n, source, target):
        copy = pltpu.make_async_copy(source, target, sems.at[n])
        copy.start()
        return copy

    loads = [
        load(0, inverse_hbm, inverse_ref),
        load(2, science_hbm, science_ref),
        load(3, weights_hbm, payload_hbm.at[:, pl.ds(BS, BS + 8), :]),
    ]
    lane = lax.broadcasted_iota(jnp.int32, (H, LANE), 1)
    across = (2.0 * lax.broadcasted_iota(jnp.int32, (H, W), 1).astype(f32) + 1.0 - W) / W
    zero = jnp.zeros((H, LANE), bf16)
    blocks_ref[NBLK] = jnp.zeros((BS, LANE), bf16)
    for v in range(VISITS):
        tiles = [(tile0_ref, tile1_ref)[v][:, b * LANE : (b + 1) * LANE] for b in range(CB)]
        for b in range(CB):
            after = tiles[b + 1] if b + 1 < CB else zero
            before = tiles[b - 1] if b > 0 else zero
            rows = pl.ds((v * CB + b) * H, H)
            window_ref[rows, pl.ds(0, LANE)] = tiles[b]
            window_ref[rows, pl.ds(LANE, LANE)] = jnp.where(lane < BS, after, before)
    for jj in range(NB // 2):
        rows = lax.dot_general(
            window_ref[...],
            band_ref[pl.ds(jj * 2 * LANE, 2 * LANE), :],
            (((1,), (1,)), ((), ())),
            preferred_element_type=f32,
        ).astype(bf16)
        for v in range(VISITS):
            for b in range(CB):
                for j in range(2):
                    top = (v * CB + b) * H
                    filtered_ref[v, pl.ds((2 * jj + j) * H, H), pl.ds(b * LANE, LANE)] = rows[
                        top : top + H, j * LANE : (j + 1) * LANE
                    ]
    for copy in loads:
        copy.wait()
    stores = []
    for v in range(VISITS):
        both = jnp.dot(both_ref[v], filtered_ref[v], preferred_element_type=f32)
        both = both[: 2 * H] + both[2 * H :]
        difference = science_ref[v] - (both[:H] + across * both[H:])
        difference_ref[v] = difference
        stores.append(load(4 + v, difference_ref.at[v], difference_hbm.at[v]))
        inverse = inverse_ref[v].astype(f32)
        spread(inverse * difference, blocks_ref, v)
    left = lax.broadcasted_iota(jnp.int32, (BS, LANE), 1) < BS
    for part in range(4):
        for o in range(part * 8, part * 8 + 8):
            source = [from_ref[2 * o + k] for k in range(2)]
            payload_ref[o] = jnp.where(left, blocks_ref[source[0]], blocks_ref[source[1]])
        owners = pl.ds(part * 8, 8)
        stores.append(load(6 + part, payload_ref.at[owners], payload_hbm.at[owners, pl.ds(0, BS), :]))
    for store in stores:
        store.wait()


def sum_kernel(arrived_ref, total_ref):
    left = lax.broadcasted_iota(jnp.int32, (BS, LANE), 1) < BS
    sums = []
    for part in range(2):
        def body(j, acc):
            head = arrived_ref[j, pl.ds(2 * BS, 8), :].astype(f32)[:1]
            value = arrived_ref[j, pl.ds(part * BS, BS), :].astype(f32)
            return tuple(
                acc[s] + jnp.where(jnp.broadcast_to(head == s, (BS, LANE)), value, 0.0) for s in range(PATCHES)
            )

        acc = lax.fori_loop(0, TILES, body, tuple(jnp.zeros((BS, LANE), f32) for _ in range(PATCHES)), unroll=4)
        sums.append([a + pltpu.roll(a, BS, 1) for a in acc])
    for s in range(PATCHES):
        total_ref[s] = jnp.where(left, sums[0][s], sums[1][s])


def final_kernel(total_ref, low_ref, high_ref, sum_ref, weight_ref, out_ref, merged_ref):
    left = lax.broadcasted_iota(jnp.int32, (BS // 2, LANE), 1) < BS
    for s in range(PATCHES):
        merged = total_ref[s]
        if s == 0:
            merged = merged + low_ref[...]
        if s == PATCHES - 1:
            merged = merged + high_ref[...]
        merged_ref[...] = merged
        even = merged_ref[pl.ds(0, BS // 2, stride=2), :]
        odd = merged_ref[pl.ds(1, BS // 2, stride=2), :]
        value = jnp.where(left, even, pltpu.roll(odd, BS, 1))
        weight = jnp.where(left, pltpu.roll(even, BS, 1), odd)
        out_ref[s] = (sum_ref[s] + value) / (weight_ref[s] + weight)


def all_to_all(x):
    return lax.all_to_all(x, "tile", split_axis=0, concat_axis=0, tiled=True)


def shards(
    science,
    inverse_variance,
    template,
    filters,
    kernel_index,
    spatial_coeff,
    visit_offset,
    block_count,
    block_owner,
    block_slot,
    coadd_sum,
    coadd_weight,
):
    sds = jax.ShapeDtypeStruct
    blocks = pltpu.VMEM((NBLK + 1, BS, LANE), bf16)
    prep = call(
        prep_kernel,
        (
            sds((NB * LANE, 2 * LANE), bf16),
            sds((8 * NB, LANE), f32),
            sds((2 * TILES,), jnp.int32),
            sds((2 * TILES,), jnp.int32),
        ),
        [SMEM] * 3 + [VMEM] * 3,
        (10_000_000, 1_000_000),
        [
            pltpu.SMEM((TILES,), jnp.int32),
            pltpu.VMEM((LANE, 2 * LANE), f32),
            pltpu.VMEM((16, LANE), f32),
        ],
        (VMEM, VMEM, SMEM, SMEM),
    )
    second_prep = call(
        second_prep_kernel,
        (sds((VISITS, 4 * H, NB * H), bf16), sds((TILES, BS + 8, LANE), bf16)),
        [SMEM, SMEM, VMEM, VMEM],
        (10_000_000, 3_000_000),
        [blocks],
    )

    def shifted(d, beside):
        pairs = [((i + d) % TILES, i) for i in range(TILES)]

        def branch(tile, args):
            return (lax.ppermute(tile, "tile", pairs) if d else tile), beside(*args)

        return branch

    own = template[0, 0]
    tables = (kernel_index.T, filters, spatial_coeff[0, 0].transpose(1, 0, 2))
    places = (block_owner[0, 0], block_slot[0, 0], block_count[0, 0])
    first, (band, eff, origin, slots) = lax.switch(
        visit_offset[0, 0], [shifted(d, prep) for d in range(TILES)], own, places + tables
    )
    second, (both, weights) = lax.switch(
        visit_offset[0, 1],
        [shifted(d, second_prep) for d in range(TILES)],
        own,
        (origin, slots, eff, inverse_variance[0, 0]),
    )

    difference, payload = call(
        main_kernel,
        (sds((VISITS, H, W), f32), sds((TILES, 2 * BS + 8, LANE), bf16)),
        [SMEM] + [VMEM] * 4 + [ANY] * 3,
        (2_000_000_000, 6_000_000),
        [
            pltpu.VMEM((VISITS * CB * H, 2 * LANE), bf16),
            pltpu.VMEM((VISITS, NB * H, W), bf16),
            blocks,
            pltpu.VMEM((VISITS, H, W), f32),
            pltpu.VMEM((VISITS, H, W), bf16),
            pltpu.VMEM((VISITS, H, W), f32),
            pltpu.VMEM((TILES, BS, LANE), bf16),
            pltpu.SemaphoreType.DMA((10,)),
        ],
        (ANY, ANY),
    )(origin, first, second, band, both, weights, science[0, 0], inverse_variance[0, 0])

    total = call(
        sum_kernel, sds((PATCHES, BS, LANE), f32), [VMEM], (5_000_000, 1_300_000)
    )(all_to_all(payload))

    count = lax.axis_size("sky")
    low = lax.ppermute(total[PATCHES - 1], "sky", [(i, i + 1) for i in range(count - 1)])
    high = lax.ppermute(total[0], "sky", [(i + 1, i) for i in range(count - 1)])
    result = call(
        final_kernel,
        sds((PATCHES, BS // 2, LANE), f32),
        [VMEM] * 5,
        (100_000, 300_000),
        [pltpu.VMEM((BS, LANE), f32)],
    )(
        total,
        low,
        high,
        coadd_sum[0, 0].reshape(PATCHES, BS // 2, LANE),
        coadd_weight[0, 0].reshape(PATCHES, BS // 2, LANE),
    )
    return (difference[None, None], result.reshape(1, 1, PATCHES, BS * BS))


def solution(mesh):
    return jax.shard_map(
        shards,
        mesh=mesh,
        in_specs=(
            P("sky", "tile", None, None, None),
            P("sky", "tile", None, None, None),
            P("sky", "tile", None, None),
            P(),
            P(),
            P("sky", "tile", None, None, None),
            P("sky", None),
            P("sky", "tile", None),
            P("sky", "tile", None),
            P("sky", "tile", None),
            P("sky", "tile", None, None),
            P("sky", "tile", None, None),
        ),
        out_specs=(P("sky", "tile", None, None, None), P("sky", "tile", None, None)),
        check_vma=False,
    )
```

```python
import jax
import jax.numpy as jnp
from jax import lax
from jax.experimental.layout import Layout, with_layout_constraint
from jax.experimental import pallas as pl
from jax.experimental.pallas import tpu as pltpu
from jax.sharding import PartitionSpec as P

TILES = 32
VISITS = 2
H = 128
W = 512
BS = 64
NB = 8
TAPS = 21
HALF = 10
LANE = 128
CB = W // LANE
NBLK = 32
BPV = NBLK // VISITS
KERNELS = 20
PATCHES = 3
f32 = jnp.float32
bf16 = jnp.bfloat16
VMEM = pl.BlockSpec(memory_space=pltpu.VMEM)
ANY = pl.BlockSpec(memory_space=pl.ANY)
SMEM = pl.BlockSpec(memory_space=pltpu.SMEM)


def call(kernel, outs, in_specs, cost, scratch=(), out_specs=None, vmem_mib=24):
    return pl.pallas_call(
        kernel,
        out_shape=outs,
        in_specs=in_specs,
        out_specs=out_specs or jax.tree.map(lambda _: VMEM, outs),
        scratch_shapes=list(scratch),
        compiler_params=pltpu.CompilerParams(vmem_limit_bytes=vmem_mib * 2**20),
        cost_estimate=pl.CostEstimate(flops=cost[0], bytes_accessed=cost[1], transcendentals=0),
    )


def toeplitz(row, width):
    return pltpu.roll(jnp.broadcast_to(row, (LANE, width)), 0, 1, stride=1, stride_axis=0)


def effective_taps(index_ref, filters_ref, coeff_ref, taps_ref, weight_ref):
    taps_ref[...] = jnp.zeros_like(taps_ref)
    taps_ref[pl.ds(0, NB), pl.ds(0, TAPS)] = filters_ref[...].astype(f32)
    taps_ref[pl.ds(0, NB), :] = pltpu.roll(taps_ref[pl.ds(0, NB), :], 2 * LANE - HALF, 1)
    weight_ref[...] = jnp.zeros_like(weight_ref)
    for v in range(VISITS):
        weight_ref[pl.ds(3 * v, 3), pl.ds(0, KERNELS)] = coeff_ref[:, v, :]
    weight_ref[pl.ds(8, 2), pl.ds(0, KERNELS)] = index_ref[...].astype(f32)
    weight = weight_ref[pl.ds(0, 8), :]
    rows = jnp.broadcast_to(weight_ref[8:9, :], (8, LANE))
    columns = jnp.broadcast_to(weight_ref[9:10, :], (LANE, LANE))
    picked = jnp.concatenate([jnp.where(rows == r, weight, 0.0) for r in range(NB)], axis=0)
    one = (lax.broadcasted_iota(jnp.int32, (LANE, LANE), 0).astype(f32) == columns).astype(f32)
    by_column = lax.dot_general(
        picked, one, (((1,), (1,)), ((), ())), precision=lax.Precision.HIGHEST, preferred_element_type=f32
    )
    taps = taps_ref[:, pl.ds(0, LANE)] + taps_ref[:, pl.ds(LANE, LANE)]
    return jnp.dot(by_column, taps, precision=lax.Precision.HIGHEST, preferred_element_type=f32)


def column_bands(eff_ref, both_ref):
    row = lax.broadcasted_iota(jnp.int32, (H, H), 0)
    inside = jnp.abs(row - lax.broadcasted_iota(jnp.int32, (H, H), 1)) <= HALF
    down = (2.0 * row.astype(f32) + 1.0 - H) / H

    def body(n, carry):
        v, r = n // NB, n % NB
        cols = pl.ds(pl.multiple_of(r * H, H), H)
        wide = [jnp.broadcast_to(eff_ref[pl.ds(8 * r + 3 * v + t, 1), :], (H, H)) for t in range(3)]
        for m, value in enumerate((wide[0] + down * wide[2], wide[1])):
            value = jnp.where(inside, pltpu.roll(value, 0, 1, stride=1, stride_axis=0), 0.0)
            high = value.astype(bf16)
            both_ref[v, pl.ds(m * H, H), cols] = high
            both_ref[v, pl.ds((2 + m) * H, H), cols] = (value - high.astype(f32)).astype(bf16)
        return carry

    lax.fori_loop(0, VISITS * NB, body, 0)


def pack_weights(from_ref, slots_ref, inverse_ref, payload_ref, blocks_ref):
    left = lax.broadcasted_iota(jnp.int32, (BS, LANE), 1) < BS
    blocks_ref[NBLK] = jnp.zeros((BS, LANE), bf16)

    def spread_pair(n, carry):
        v, by, pair = n // 8, n // CB % 2, n % CB
        here = inverse_ref[
            v, pl.ds(pl.multiple_of(by * BS, BS), BS), pl.ds(pl.multiple_of(pair * LANE, LANE), LANE)
        ].astype(f32)
        there = pltpu.roll(here, BS, 1)
        blocks_ref[2 * n] = jnp.where(left, here, there).astype(bf16)
        blocks_ref[2 * n + 1] = jnp.where(left, there, here).astype(bf16)
        return carry

    lax.fori_loop(0, NBLK // 2, spread_pair, 0)

    def place(o, carry):
        payload_ref[o, pl.ds(0, BS), :] = jnp.where(
            left, blocks_ref[from_ref[2 * o]], blocks_ref[from_ref[2 * o + 1]]
        )
        slots = [jnp.full((8, LANE), slots_ref[2 * o + k], jnp.int32) for k in range(2)]
        payload_ref[o, pl.ds(BS, 8), :] = jnp.where(left[:8], slots[0], slots[1]).astype(f32).astype(bf16)
        return carry

    lax.fori_loop(0, TILES, place, 0, unroll=2)


def prep_kernel(
    owner_ref, slot_ref, count_ref, index_ref, filters_ref, coeff_ref,
    eff_ref, taps_ref, from_ref, slots_ref, seen_ref, weight_ref,
):
    def clear(o, carry):
        from_ref[2 * o] = NBLK
        from_ref[2 * o + 1] = NBLK
        slots_ref[2 * o] = 0
        slots_ref[2 * o + 1] = 0
        seen_ref[o] = 0
        return carry

    lax.fori_loop(0, TILES, clear, 0, unroll=4)
    eff_ref[...] = effective_taps(index_ref, filters_ref, coeff_ref, taps_ref, weight_ref)
    for v in range(VISITS):
        count = count_ref[v]

        def put(i, carry, v=v, count=count):
            r = v * BPV + i
            owner = owner_ref[r]
            repeat = seen_ref[owner]
            seen_ref[owner] = repeat + 1
            place = 2 * owner + repeat
            from_ref[place] = jnp.where(i < count, r, NBLK)
            slots_ref[place] = slot_ref[r]
            return carry

        lax.fori_loop(0, BPV, put, 0, unroll=2)


def second_prep_kernel(
    from_ref, slots_ref, eff_ref, taps_ref, inverse_ref, band_ref, both_ref, payload_ref, blocks_ref
):
    def band(j, carry):
        rows = pl.ds(pl.multiple_of(j * LANE, LANE), LANE)
        band_ref[rows, :] = toeplitz(taps_ref[pl.ds(j, 1), :], 2 * LANE).astype(bf16)
        return carry

    lax.fori_loop(0, NB, band, 0, unroll=2)
    column_bands(eff_ref, both_ref)
    pack_weights(from_ref, slots_ref, inverse_ref, payload_ref, blocks_ref)


def spread(plane, blocks_ref, v):
    left = lax.broadcasted_iota(jnp.int32, (BS, LANE), 1) < BS
    for by in range(H // BS):
        for pair in range(CB):
            here = plane[by * BS : (by + 1) * BS, pair * LANE : (pair + 1) * LANE]
            there = pltpu.roll(here, BS, 1)
            r = v * BPV + by * (W // BS) + pair * 2
            blocks_ref[r] = jnp.where(left, here, there).astype(bf16)
            blocks_ref[r + 1] = jnp.where(left, there, here).astype(bf16)


def stay_kernel(tile_hbm, out_hbm, sem):
    copy = pltpu.make_async_copy(tile_hbm, out_hbm, sem)
    copy.start()
    copy.wait()


def main_kernel(
    from_ref, tile0_ref, tile1_ref, band_ref, both_ref, weights_hbm, science_hbm, inverse_hbm,
    difference_hbm, payload_hbm, window_ref, filtered_ref, blocks_ref,
    science_ref, inverse_ref, difference_ref, payload_ref, sems,
):
    def load(n, source, target):
        copy = pltpu.make_async_copy(source, target, sems.at[n])
        copy.start()
        return copy

    loads = [
        load(0, inverse_hbm, inverse_ref),
        load(2, science_hbm, science_ref),
        load(3, weights_hbm, payload_hbm.at[:, pl.ds(BS, BS + 8), :]),
    ]
    lane = lax.broadcasted_iota(jnp.int32, (H, LANE), 1)
    across = (2.0 * lax.broadcasted_iota(jnp.int32, (H, W), 1).astype(f32) + 1.0 - W) / W
    zero = jnp.zeros((H, LANE), bf16)
    blocks_ref[NBLK] = jnp.zeros((BS, LANE), bf16)
    for v in range(VISITS):
        tiles = [(tile0_ref, tile1_ref)[v][:, b * LANE : (b + 1) * LANE] for b in range(CB)]
        for b in range(CB):
            after = tiles[b + 1] if b + 1 < CB else zero
            before = tiles[b - 1] if b > 0 else zero
            rows = pl.ds((v * CB + b) * H, H)
            window_ref[rows, pl.ds(0, LANE)] = tiles[b]
            window_ref[rows, pl.ds(LANE, LANE)] = jnp.where(lane < BS, after, before)
    for jj in range(NB // 2):
        rows = lax.dot_general(
            window_ref[...],
            band_ref[pl.ds(jj * 2 * LANE, 2 * LANE), :],
            (((1,), (1,)), ((), ())),
            preferred_element_type=f32,
        ).astype(bf16)
        for v in range(VISITS):
            for b in range(CB):
                for j in range(2):
                    top = (v * CB + b) * H
                    filtered_ref[v, pl.ds((2 * jj + j) * H, H), pl.ds(b * LANE, LANE)] = rows[
                        top : top + H, j * LANE : (j + 1) * LANE
                    ]
    for copy in loads[:-1]:
        copy.wait()
    stores = loads[-1:]
    for v in range(VISITS):
        both = jnp.dot(both_ref[v], filtered_ref[v], preferred_element_type=f32)
        both = both[: 2 * H] + both[2 * H :]
        difference = science_ref[v] - (both[:H] + across * both[H:])
        difference_ref[v] = difference
        stores.append(load(4 + v, difference_ref.at[v], difference_hbm.at[v]))
        inverse = inverse_ref[v].astype(f32)
        spread(inverse * difference, blocks_ref, v)
    left = lax.broadcasted_iota(jnp.int32, (BS, LANE), 1) < BS
    for part in range(4):
        for o in range(part * 8, part * 8 + 8):
            source = [from_ref[2 * o + k] for k in range(2)]
            payload_ref[o] = jnp.where(left, blocks_ref[source[0]], blocks_ref[source[1]])
        owners = pl.ds(part * 8, 8)
        stores.append(load(6 + part, payload_ref.at[owners], payload_hbm.at[owners, pl.ds(0, BS), :]))
    for store in stores:
        store.wait()


def sum_kernel(arrived_ref, total_ref):
    left = lax.broadcasted_iota(jnp.int32, (BS, LANE), 1) < BS
    sums = []
    for part in range(2):
        def body(j, acc):
            head = arrived_ref[j, pl.ds(2 * BS, 8), :].astype(f32)[:1]
            value = arrived_ref[j, pl.ds(part * BS, BS), :].astype(f32)
            return tuple(
                acc[s] + jnp.where(jnp.broadcast_to(head == s, (BS, LANE)), value, 0.0) for s in range(PATCHES)
            )

        acc = lax.fori_loop(0, TILES, body, tuple(jnp.zeros((BS, LANE), f32) for _ in range(PATCHES)), unroll=4)
        sums.append([a + pltpu.roll(a, BS, 1) for a in acc])
    for s in range(PATCHES):
        total_ref[s] = jnp.where(left, sums[0][s], sums[1][s])


def final_kernel(total_ref, low_ref, high_ref, sum_ref, weight_ref, out_ref, merged_ref):
    left = lax.broadcasted_iota(jnp.int32, (BS // 2, LANE), 1) < BS
    for s in range(PATCHES):
        merged = total_ref[s]
        if s == 0:
            merged = merged + low_ref[...]
        if s == PATCHES - 1:
            merged = merged + high_ref[...]
        merged_ref[...] = merged
        even = merged_ref[pl.ds(0, BS // 2, stride=2), :]
        odd = merged_ref[pl.ds(1, BS // 2, stride=2), :]
        value = jnp.where(left, even, pltpu.roll(odd, BS, 1))
        weight = jnp.where(left, pltpu.roll(even, BS, 1), odd)
        out_ref[s] = (sum_ref[s] + value) / (weight_ref[s] + weight)


def all_to_all(x):
    return lax.all_to_all(x, "tile", split_axis=0, concat_axis=0, tiled=True)


def shards(
    science,
    inverse_variance,
    template,
    filters,
    kernel_index,
    spatial_coeff,
    visit_offset,
    block_count,
    block_owner,
    block_slot,
    coadd_sum,
    coadd_weight,
):
    sds = jax.ShapeDtypeStruct
    blocks = pltpu.VMEM((NBLK + 1, BS, LANE), bf16)
    prep = call(
        prep_kernel,
        (
            sds((8 * NB, LANE), f32),
            sds((LANE, 2 * LANE), f32),
            sds((2 * TILES,), jnp.int32),
            sds((2 * TILES,), jnp.int32),
        ),
        [SMEM] * 3 + [VMEM] * 3,
        (10_000_000, 1_000_000),
        [
            pltpu.SMEM((TILES,), jnp.int32),
            pltpu.VMEM((16, LANE), f32),
        ],
        (VMEM, VMEM, SMEM, SMEM),
    )
    second_prep = call(
        second_prep_kernel,
        (
            sds((NB * LANE, 2 * LANE), bf16),
            sds((VISITS, 4 * H, NB * H), bf16),
            sds((TILES, BS + 8, LANE), bf16),
        ),
        [SMEM, SMEM] + [VMEM] * 3,
        (10_000_000, 3_000_000),
        [blocks],
    )

    stay = call(
        stay_kernel, sds((H, W), bf16), [ANY], (0, 300_000), [pltpu.SemaphoreType.DMA], ANY
    )

    def shifted(d, beside):
        pairs = [((i + d) % TILES, i) for i in range(TILES)]

        def branch(tile, args):
            return (lax.ppermute(tile, "tile", pairs) if d else stay(tile)), beside(*args)

        return branch

    own = template[0, 0]
    tables = (kernel_index.T, filters, spatial_coeff[0, 0].transpose(1, 0, 2))
    places = (block_owner[0, 0], block_slot[0, 0], block_count[0, 0])
    first, (eff, taps, origin, slots) = lax.switch(
        visit_offset[0, 0], [shifted(d, prep) for d in range(TILES)], own, places + tables
    )
    second, (band, both, weights) = lax.switch(
        visit_offset[0, 1],
        [shifted(d, second_prep) for d in range(TILES)],
        own,
        (origin, slots, eff, taps, inverse_variance[0, 0]),
    )

    difference, payload = call(
        main_kernel,
        (sds((VISITS, H, W), f32), sds((TILES, 2 * BS + 8, LANE), bf16)),
        [SMEM] + [VMEM] * 4 + [ANY] * 3,
        (2_000_000_000, 6_000_000),
        [
            pltpu.VMEM((VISITS * CB * H, 2 * LANE), bf16),
            pltpu.VMEM((VISITS, NB * H, W), bf16),
            blocks,
            pltpu.VMEM((VISITS, H, W), f32),
            pltpu.VMEM((VISITS, H, W), bf16),
            pltpu.VMEM((VISITS, H, W), f32),
            pltpu.VMEM((TILES, BS, LANE), bf16),
            pltpu.SemaphoreType.DMA((10,)),
        ],
        (ANY, ANY),
    )(origin, first, second, band, both, weights, science[0, 0], inverse_variance[0, 0])

    total = call(
        sum_kernel, sds((PATCHES, BS, LANE), f32), [VMEM], (5_000_000, 1_300_000)
    )(all_to_all(payload))

    count = lax.axis_size("sky")
    low = lax.ppermute(total[PATCHES - 1], "sky", [(i, i + 1) for i in range(count - 1)])
    high = lax.ppermute(total[0], "sky", [(i + 1, i) for i in range(count - 1)])
    result = call(
        final_kernel,
        sds((PATCHES, BS // 2, LANE), f32),
        [VMEM] * 5,
        (100_000, 300_000),
        [pltpu.VMEM((BS, LANE), f32)],
    )(
        total,
        low,
        high,
        coadd_sum[0, 0].reshape(PATCHES, BS // 2, LANE),
        coadd_weight[0, 0].reshape(PATCHES, BS // 2, LANE),
    )
    return (difference[None, None], result.reshape(1, 1, PATCHES, BS * BS))


def solution(mesh):
    return jax.shard_map(
        shards,
        mesh=mesh,
        in_specs=(
            P("sky", "tile", None, None, None),
            P("sky", "tile", None, None, None),
            P("sky", "tile", None, None),
            P(),
            P(),
            P("sky", "tile", None, None, None),
            P("sky", None),
            P("sky", "tile", None),
            P("sky", "tile", None),
            P("sky", "tile", None),
            P("sky", "tile", None, None),
            P("sky", "tile", None, None),
        ),
        out_specs=(P("sky", "tile", None, None, None), P("sky", "tile", None, None)),
        check_vma=False,
    )
```

```python
import jax
import jax.numpy as jnp
from jax import lax
from jax.experimental.layout import Layout, with_layout_constraint
from jax.experimental import pallas as pl
from jax.experimental.pallas import tpu as pltpu
from jax.sharding import PartitionSpec as P

TILES = 32
VISITS = 2
H = 128
W = 512
BS = 64
NB = 8
TAPS = 21
HALF = 10
LANE = 128
CB = W // LANE
NBLK = 32
BPV = NBLK // VISITS
KERNELS = 20
PATCHES = 3
f32 = jnp.float32
bf16 = jnp.bfloat16
VMEM = pl.BlockSpec(memory_space=pltpu.VMEM)
ANY = pl.BlockSpec(memory_space=pl.ANY)
SMEM = pl.BlockSpec(memory_space=pltpu.SMEM)


def call(kernel, outs, in_specs, cost, scratch=(), out_specs=None, vmem_mib=24):
    return pl.pallas_call(
        kernel,
        out_shape=outs,
        in_specs=in_specs,
        out_specs=out_specs or jax.tree.map(lambda _: VMEM, outs),
        scratch_shapes=list(scratch),
        compiler_params=pltpu.CompilerParams(vmem_limit_bytes=vmem_mib * 2**20),
        cost_estimate=pl.CostEstimate(flops=cost[0], bytes_accessed=cost[1], transcendentals=0),
    )


def toeplitz(row, width):
    return pltpu.roll(jnp.broadcast_to(row, (LANE, width)), 0, 1, stride=1, stride_axis=0)


def effective_taps(index_ref, filters_ref, coeff_ref, taps_ref, weight_ref):
    taps_ref[...] = jnp.zeros_like(taps_ref)
    taps_ref[pl.ds(0, NB), pl.ds(0, TAPS)] = filters_ref[...].astype(f32)
    taps_ref[pl.ds(0, NB), :] = pltpu.roll(taps_ref[pl.ds(0, NB), :], 2 * LANE - HALF, 1)
    weight_ref[...] = jnp.zeros_like(weight_ref)
    for v in range(VISITS):
        weight_ref[pl.ds(3 * v, 3), pl.ds(0, KERNELS)] = coeff_ref[:, v, :]
    weight_ref[pl.ds(8, 2), pl.ds(0, KERNELS)] = index_ref[...].astype(f32)
    weight = weight_ref[pl.ds(0, 8), :]
    rows = jnp.broadcast_to(weight_ref[8:9, :], (8, LANE))
    columns = jnp.broadcast_to(weight_ref[9:10, :], (LANE, LANE))
    picked = jnp.concatenate([jnp.where(rows == r, weight, 0.0) for r in range(NB)], axis=0)
    one = (lax.broadcasted_iota(jnp.int32, (LANE, LANE), 0).astype(f32) == columns).astype(f32)
    by_column = lax.dot_general(
        picked, one, (((1,), (1,)), ((), ())), precision=lax.Precision.HIGHEST, preferred_element_type=f32
    )
    taps = taps_ref[:, pl.ds(0, LANE)] + taps_ref[:, pl.ds(LANE, LANE)]
    return jnp.dot(by_column, taps, precision=lax.Precision.HIGHEST, preferred_element_type=f32)


def column_bands(eff_ref, both_ref):
    row = lax.broadcasted_iota(jnp.int32, (H, H), 0)
    inside = jnp.abs(row - lax.broadcasted_iota(jnp.int32, (H, H), 1)) <= HALF
    down = (2.0 * row.astype(f32) + 1.0 - H) / H

    def body(n, carry):
        v, r = n // NB, n % NB
        cols = pl.ds(pl.multiple_of(r * H, H), H)
        wide = [jnp.broadcast_to(eff_ref[pl.ds(8 * r + 3 * v + t, 1), :], (H, H)) for t in range(3)]
        for m, value in enumerate((wide[0] + down * wide[2], wide[1])):
            value = jnp.where(inside, pltpu.roll(value, 0, 1, stride=1, stride_axis=0), 0.0)
            high = value.astype(bf16)
            both_ref[v, pl.ds(m * H, H), cols] = high
            both_ref[v, pl.ds((2 + m) * H, H), cols] = (value - high.astype(f32)).astype(bf16)
        return carry

    lax.fori_loop(0, VISITS * NB, body, 0)


def pack_weights(from_ref, slots_ref, inverse_ref, payload_ref, blocks_ref):
    left = lax.broadcasted_iota(jnp.int32, (BS, LANE), 1) < BS
    blocks_ref[NBLK] = jnp.zeros((BS, LANE), bf16)

    def spread_pair(n, carry):
        v, by, pair = n // 8, n // CB % 2, n % CB
        here = inverse_ref[
            v, pl.ds(pl.multiple_of(by * BS, BS), BS), pl.ds(pl.multiple_of(pair * LANE, LANE), LANE)
        ].astype(f32)
        there = pltpu.roll(here, BS, 1)
        blocks_ref[2 * n] = jnp.where(left, here, there).astype(bf16)
        blocks_ref[2 * n + 1] = jnp.where(left, there, here).astype(bf16)
        return carry

    lax.fori_loop(0, NBLK // 2, spread_pair, 0)

    def place(o, carry):
        payload_ref[o, pl.ds(0, BS), :] = jnp.where(
            left, blocks_ref[from_ref[2 * o]], blocks_ref[from_ref[2 * o + 1]]
        )
        slots = [jnp.full((8, LANE), slots_ref[2 * o + k], jnp.int32) for k in range(2)]
        payload_ref[o, pl.ds(BS, 8), :] = jnp.where(left[:8], slots[0], slots[1]).astype(f32).astype(bf16)
        return carry

    lax.fori_loop(0, TILES, place, 0, unroll=2)


def prep_kernel(
    owner_ref, slot_ref, count_ref, index_ref, filters_ref, coeff_ref,
    eff_ref, taps_ref, from_ref, slots_ref, seen_ref, weight_ref,
):
    def clear(o, carry):
        from_ref[2 * o] = NBLK
        from_ref[2 * o + 1] = NBLK
        slots_ref[2 * o] = 0
        slots_ref[2 * o + 1] = 0
        seen_ref[o] = 0
        return carry

    lax.fori_loop(0, TILES, clear, 0, unroll=4)
    eff_ref[...] = effective_taps(index_ref, filters_ref, coeff_ref, taps_ref, weight_ref)
    for v in range(VISITS):
        count = count_ref[v]

        def put(i, carry, v=v, count=count):
            r = v * BPV + i
            owner = owner_ref[r]
            repeat = seen_ref[owner]
            seen_ref[owner] = repeat + 1
            place = 2 * owner + repeat
            from_ref[place] = jnp.where(i < count, r, NBLK)
            slots_ref[place] = slot_ref[r]
            return carry

        lax.fori_loop(0, BPV, put, 0, unroll=2)


def second_prep_kernel(
    from_ref, slots_ref, eff_ref, taps_ref, inverse_ref, band_ref, both_ref, payload_ref, blocks_ref
):
    def band(j, carry):
        rows = pl.ds(pl.multiple_of(j * LANE, LANE), LANE)
        band_ref[rows, :] = toeplitz(taps_ref[pl.ds(j, 1), :], 2 * LANE).astype(bf16)
        return carry

    lax.fori_loop(0, NB, band, 0, unroll=2)
    column_bands(eff_ref, both_ref)
    pack_weights(from_ref, slots_ref, inverse_ref, payload_ref, blocks_ref)


def spread(plane, blocks_ref, v):
    left = lax.broadcasted_iota(jnp.int32, (BS, LANE), 1) < BS
    for by in range(H // BS):
        for pair in range(CB):
            here = plane[by * BS : (by + 1) * BS, pair * LANE : (pair + 1) * LANE]
            there = pltpu.roll(here, BS, 1)
            r = v * BPV + by * (W // BS) + pair * 2
            blocks_ref[r] = jnp.where(left, here, there).astype(bf16)
            blocks_ref[r + 1] = jnp.where(left, there, here).astype(bf16)


def stay_kernel(tile_ref, out_ref):
    out_ref[...] = tile_ref[...]


def main_kernel(
    from_ref, tile0_ref, tile1_ref, band_ref, both_ref, weights_hbm, science_hbm, inverse_hbm,
    difference_hbm, payload_hbm, window_ref, filtered_ref, blocks_ref,
    science_ref, inverse_ref, difference_ref, payload_ref, sems,
):
    def load(n, source, target):
        copy = pltpu.make_async_copy(source, target, sems.at[n])
        copy.start()
        return copy

    loads = [
        load(0, inverse_hbm, inverse_ref),
        load(2, science_hbm, science_ref),
        load(3, weights_hbm, payload_hbm.at[:, pl.ds(BS, BS + 8), :]),
    ]
    lane = lax.broadcasted_iota(jnp.int32, (H, LANE), 1)
    across = (2.0 * lax.broadcasted_iota(jnp.int32, (H, W), 1).astype(f32) + 1.0 - W) / W
    zero = jnp.zeros((H, LANE), bf16)
    blocks_ref[NBLK] = jnp.zeros((BS, LANE), bf16)
    for v in range(VISITS):
        tiles = [(tile0_ref, tile1_ref)[v][:, b * LANE : (b + 1) * LANE] for b in range(CB)]
        for b in range(CB):
            after = tiles[b + 1] if b + 1 < CB else zero
            before = tiles[b - 1] if b > 0 else zero
            rows = pl.ds((v * CB + b) * H, H)
            window_ref[rows, pl.ds(0, LANE)] = tiles[b]
            window_ref[rows, pl.ds(LANE, LANE)] = jnp.where(lane < BS, after, before)
    for jj in range(NB // 2):
        rows = lax.dot_general(
            window_ref[...],
            band_ref[pl.ds(jj * 2 * LANE, 2 * LANE), :],
            (((1,), (1,)), ((), ())),
            preferred_element_type=f32,
        ).astype(bf16)
        for v in range(VISITS):
            for b in range(CB):
                for j in range(2):
                    top = (v * CB + b) * H
                    filtered_ref[v, pl.ds((2 * jj + j) * H, H), pl.ds(b * LANE, LANE)] = rows[
                        top : top + H, j * LANE : (j + 1) * LANE
                    ]
    for copy in loads[:-1]:
        copy.wait()
    stores = loads[-1:]
    for v in range(VISITS):
        both = jnp.dot(both_ref[v], filtered_ref[v], preferred_element_type=f32)
        both = both[: 2 * H] + both[2 * H :]
        difference = science_ref[v] - (both[:H] + across * both[H:])
        difference_ref[v] = difference
        stores.append(load(4 + v, difference_ref.at[v], difference_hbm.at[v]))
        inverse = inverse_ref[v].astype(f32)
        spread(inverse * difference, blocks_ref, v)
    left = lax.broadcasted_iota(jnp.int32, (BS, LANE), 1) < BS
    for part in range(4):
        for o in range(part * 8, part * 8 + 8):
            source = [from_ref[2 * o + k] for k in range(2)]
            payload_ref[o] = jnp.where(left, blocks_ref[source[0]], blocks_ref[source[1]])
        owners = pl.ds(part * 8, 8)
        stores.append(load(6 + part, payload_ref.at[owners], payload_hbm.at[owners, pl.ds(0, BS), :]))
    for store in stores:
        store.wait()


def sum_kernel(arrived_ref, *total_refs):
    left = lax.broadcasted_iota(jnp.int32, (BS, LANE), 1) < BS
    sums = []
    for part in range(2):
        def body(j, acc):
            head = jnp.broadcast_to(arrived_ref[j, pl.ds(2 * BS, 8), :].astype(f32)[:1], (BS, LANE))
            value = arrived_ref[j, pl.ds(part * BS, BS), :].astype(f32)
            return tuple(acc[s] + jnp.where(head == s, value, 0.0) for s in range(PATCHES))

        acc = lax.fori_loop(0, TILES, body, tuple(jnp.zeros((BS, LANE), f32) for _ in range(PATCHES)), unroll=8)
        sums.append([a + pltpu.roll(a, BS, 1) for a in acc])
    for s in range(PATCHES):
        total_refs[s][...] = jnp.where(left, sums[0][s], sums[1][s])


def final_kernel(first_ref, middle_ref, last_ref, low_ref, high_ref, sum_ref, weight_ref, out_ref, merged_ref):
    left = lax.broadcasted_iota(jnp.int32, (BS // 2, LANE), 1) < BS
    for s in range(PATCHES):
        merged = (first_ref, middle_ref, last_ref)[s][...]
        if s == 0:
            merged = merged + low_ref[...]
        if s == PATCHES - 1:
            merged = merged + high_ref[...]
        merged_ref[...] = merged
        even = merged_ref[pl.ds(0, BS // 2, stride=2), :]
        odd = merged_ref[pl.ds(1, BS // 2, stride=2), :]
        value = jnp.where(left, even, pltpu.roll(odd, BS, 1))
        weight = jnp.where(left, pltpu.roll(even, BS, 1), odd)
        out_ref[s] = (sum_ref[s] + value) / (weight_ref[s] + weight)


def all_to_all(x):
    return lax.all_to_all(x, "tile", split_axis=0, concat_axis=0, tiled=True)


def shards(
    science,
    inverse_variance,
    template,
    filters,
    kernel_index,
    spatial_coeff,
    visit_offset,
    block_count,
    block_owner,
    block_slot,
    coadd_sum,
    coadd_weight,
):
    sds = jax.ShapeDtypeStruct
    blocks = pltpu.VMEM((NBLK + 1, BS, LANE), bf16)
    prep = call(
        prep_kernel,
        (
            sds((8 * NB, LANE), f32),
            sds((LANE, 2 * LANE), f32),
            sds((2 * TILES,), jnp.int32),
            sds((2 * TILES,), jnp.int32),
        ),
        [SMEM] * 3 + [VMEM] * 3,
        (10_000_000, 1_000_000),
        [
            pltpu.SMEM((TILES,), jnp.int32),
            pltpu.VMEM((16, LANE), f32),
        ],
        (VMEM, VMEM, SMEM, SMEM),
    )
    second_prep = call(
        second_prep_kernel,
        (
            sds((NB * LANE, 2 * LANE), bf16),
            sds((VISITS, 4 * H, NB * H), bf16),
            sds((TILES, BS + 8, LANE), bf16),
        ),
        [SMEM, SMEM] + [VMEM] * 3,
        (10_000_000, 3_000_000),
        [blocks],
    )

    stay = call(
        stay_kernel, sds((H, W), bf16), [VMEM], (0, 300_000)
    )

    def shifted(d, beside):
        pairs = [((i + d) % TILES, i) for i in range(TILES)]

        def branch(tile, args):
            return (lax.ppermute(tile, "tile", pairs) if d else stay(tile)), beside(*args)

        return branch

    own = template[0, 0]
    tables = (kernel_index.T, filters, spatial_coeff[0, 0].transpose(1, 0, 2))
    places = (block_owner[0, 0], block_slot[0, 0], block_count[0, 0])
    first, (eff, taps, origin, slots) = lax.switch(
        visit_offset[0, 0], [shifted(d, prep) for d in range(TILES)], own, places + tables
    )
    second, (band, both, weights) = lax.switch(
        visit_offset[0, 1],
        [shifted(d, second_prep) for d in range(TILES)],
        own,
        (origin, slots, eff, taps, inverse_variance[0, 0]),
    )

    difference, payload = call(
        main_kernel,
        (sds((VISITS, H, W), f32), sds((TILES, 2 * BS + 8, LANE), bf16)),
        [SMEM] + [VMEM] * 4 + [ANY] * 3,
        (2_000_000_000, 6_000_000),
        [
            pltpu.VMEM((VISITS * CB * H, 2 * LANE), bf16),
            pltpu.VMEM((VISITS, NB * H, W), bf16),
            blocks,
            pltpu.VMEM((VISITS, H, W), f32),
            pltpu.VMEM((VISITS, H, W), bf16),
            pltpu.VMEM((VISITS, H, W), f32),
            pltpu.VMEM((TILES, BS, LANE), bf16),
            pltpu.SemaphoreType.DMA((10,)),
        ],
        (ANY, ANY),
    )(origin, first, second, band, both, weights, science[0, 0], inverse_variance[0, 0])

    total = call(
        sum_kernel, (sds((BS, LANE), f32),) * PATCHES, [VMEM], (5_000_000, 1_300_000)
    )(all_to_all(payload))

    count = lax.axis_size("sky")
    low = lax.ppermute(total[-1], "sky", [(i, i + 1) for i in range(count - 1)])
    high = lax.ppermute(total[0], "sky", [(i + 1, i) for i in range(count - 1)])
    result = call(
        final_kernel,
        sds((PATCHES, BS // 2, LANE), f32),
        [VMEM] * 7,
        (100_000, 300_000),
        [pltpu.VMEM((BS, LANE), f32)],
    )(
        *total,
        low,
        high,
        coadd_sum[0, 0].reshape(PATCHES, BS // 2, LANE),
        coadd_weight[0, 0].reshape(PATCHES, BS // 2, LANE),
    )
    return (difference[None, None], result.reshape(1, 1, PATCHES, BS * BS))


def solution(mesh):
    return jax.shard_map(
        shards,
        mesh=mesh,
        in_specs=(
            P("sky", "tile", None, None, None),
            P("sky", "tile", None, None, None),
            P("sky", "tile", None, None),
            P(),
            P(),
            P("sky", "tile", None, None, None),
            P("sky", None),
            P("sky", "tile", None),
            P("sky", "tile", None),
            P("sky", "tile", None),
            P("sky", "tile", None, None),
            P("sky", "tile", None, None),
        ),
        out_specs=(P("sky", "tile", None, None, None), P("sky", "tile", None, None)),
        check_vma=False,
    )
```
